32 devices in a mesh: row: 4 (over y, x), col: 8 (over z, core).
Axes of the slice: x: 2, y: 2, z: 4, core: 2. Of those that a mesh axis runs over, the one named last changes fastest.
Arguments:
- specimen: float32 [2, 2048, 4096], P(None, 'row', 'col'), may hold values from -1 to 2, as said below
- probe_field: float32 [2, 256, 256], replicated, may hold values from -6 to 6
- measured: float32 [4, 8, 8, 256, 256], P('row', 'col'), may hold values from 0 to 4
- offsets: int32 [4, 8, 8, 2], P('row', 'col'), may hold values from 0 to 511
- live_counts: int32 [4, 8], P('row', 'col'), may hold values from 1 to 8, as said below
Outputs:
- specimen_grad: float32 [2, 2048, 4096], P(None, 'row', 'col')
- probe_step: float32 [2, 256, 256], replicated
The draws below stay inside these ranges and needn't reach their ends.
Inputs may be any that keep to these rules, and one draw needn't show every extreme that they name: `specimen`: real parts lie in 0.5 to 2 and imaginary parts in -1 to 1. `live_counts`: some device has all 8 slots live.
All inputs are finite; a program needn't handle non-finite values.
Results may differ from the reference program's by a relative error of at most 0.0003.
Values sent between devices are 32-bit elements; how exact they have to be, the bound alone decides.
No kernel may reach another device: no remote copies, remote signals or barrier semaphores. Data moves between devices by JAX's collectives and lax.ppermute only.
A program may use at most 128 MiB of HBM per device.

```python
import math
import jax
import jax.numpy as jnp
from jax import lax

W = 256
TILE = 512
SLOTS = 8
NR = 2048
NC = 4096
N_ROW = 4
N_COL = 8


def draw_specimen(key, part):
    key_real = jax.random.fold_in(key, 11)
    key_imag = jax.random.fold_in(key, 12)
    real_part = jax.random.uniform(key_real, (NR, NC), jnp.float32, 0.5, 1.5)
    imag_part = jax.random.uniform(key_imag, (NR, NC), jnp.float32, -0.5, 0.5)
    return jnp.stack([real_part, imag_part]).astype(jnp.float32)


def draw_live_counts(key, part):
    key_counts = jax.random.fold_in(key, 21)
    key_pick = jax.random.fold_in(key, 22)
    counts = jax.random.randint(key_counts, (N_ROW * N_COL,), 1, SLOTS + 1, jnp.int32)
    chosen = jax.random.randint(key_pick, (), 0, N_ROW * N_COL, jnp.int32)
    counts = counts.at[chosen].set(SLOTS)
    return counts.reshape(N_ROW, N_COL)


def touch_ends(entries, rng, least, high):
    dims = entries.shape
    spot = [jax.random.randint(jax.random.fold_in(rng, axis), (), 0, dims[axis]) for axis in range(len(dims))]
    entries = entries.at[tuple(spot)].set(least)
    longest = dims.index(max(dims))
    spot[longest] = (spot[longest] + 1) % dims[longest]
    return entries.at[tuple(spot)].set(high)


def level_of(own_key, dims, split, least, top_value):
    def one(position, parts):
        draws = jax.random.uniform(jax.random.fold_in(jax.random.fold_in(own_key, 6), position), (parts,), jnp.float32, least / len(split), top_value / len(split))
        return jnp.repeat(jnp.exp(draws), dims[position] // parts).reshape((-1,) + (1,) * (len(dims) - position - 1))

    loudness = one(*split[0])
    for cut in split[1:]:
        loudness = loudness * one(*cut)
    return loudness


def gaussian(stream_key, extent, width, limit, kind=jnp.bfloat16):
    entries = width * jax.random.normal(stream_key, extent, jnp.float32)
    return jnp.clip(entries, min=-limit, max=limit).astype(kind)


def setup_inputs(seed: int = 0) -> dict:
    seeds = jax.random.split(jax.random.key(seed), 6)
    return {
        "specimen": draw_specimen(jax.random.fold_in(seeds[5], 71), 0),
        "probe_field": gaussian(seeds[1], (2, W, W), 1.0, 6.0, jnp.float32),
        "measured": jnp.clip(4.0 * jax.random.uniform(seeds[2], (N_ROW, N_COL, SLOTS, W, W), jnp.float32) ** level_of(seeds[2], (N_ROW, N_COL, SLOTS, W, W), ((0, 4), (1, 8)), -0.2, 0.2), 0.0, 4.0),
        "offsets": touch_ends(jax.random.randint(seeds[3], (N_ROW, N_COL, SLOTS, 2), 0, TILE), jax.random.fold_in(seeds[3], 1), 0, TILE - 1).astype(jnp.int32),
        "live_counts": draw_live_counts(jax.random.fold_in(seeds[5], 71), 0),
    }


near_field = 0.25

def chirp_phase():
    index_range = jnp.arange(W)
    wave_number = jnp.where(index_range < W // 2, index_range, index_range - W).astype(jnp.float32)
    squared = wave_number[:, None] ** 2 + wave_number[None, :] ** 2
    return -math.pi * near_field * squared / W

def reference(specimen, probe_field, measured, offsets, live_counts):
    whole = specimen[0] + 1j * specimen[1]
    probe_c = probe_field[0] + 1j * probe_field[1]
    phase = chirp_phase()
    forward_chirp = jnp.exp(1j * phase)
    backward_chirp = jnp.exp(-1j * phase)
    total = N_ROW * N_COL * SLOTS
    flat_index = jnp.arange(total).astype(jnp.int32)
    dev_row = flat_index // (N_COL * SLOTS)
    dev_col = flat_index // SLOTS % N_COL
    slot_index = flat_index % SLOTS
    flat_offsets = offsets.reshape(total, 2)
    flat_measured = measured.reshape(total, W, W)
    pixel = jnp.arange(W).astype(jnp.int32)

    def step(carry, batch_entry):
        grad_c, probe_sum, illum = carry
        row_delta, column_delta, slot_delta, patch_corner, observed_intensity = batch_entry
        row_idx = (row_delta * TILE + patch_corner[0] + pixel) % NR
        col_idx = (column_delta * TILE + patch_corner[1] + pixel) % NC
        window = whole[row_idx[:, None], col_idx[None, :]]
        active_mask = (slot_delta < live_counts[row_delta, column_delta]).astype(jnp.float32)
        wave = jnp.fft.ifft2(jnp.fft.fft2(probe_c * window) * forward_chirp)
        model_intensity = wave.real ** 2 + wave.imag ** 2
        amplitude_residual = active_mask * (model_intensity - observed_intensity)
        back = jnp.fft.ifft2(jnp.fft.fft2(amplitude_residual * wave) * backward_chirp)
        grad_c = grad_c.at[row_idx[:, None], col_idx[None, :]].add(jnp.conj(probe_c) * back)
        probe_sum = probe_sum + jnp.conj(window) * back
        illum = illum + active_mask * (window.real ** 2 + window.imag ** 2)
        return ((grad_c, probe_sum, illum), None)
    start = (jnp.zeros(whole.shape, whole.dtype), jnp.zeros(probe_c.shape, probe_c.dtype), jnp.zeros((W, W), jnp.float32))
    (grad_c, probe_sum, illum), _ = lax.scan(step, start, (dev_row, dev_col, slot_index, flat_offsets, flat_measured))
    specimen_grad = jnp.stack([grad_c.real, grad_c.imag])
    root = jnp.sqrt(illum)
    probe_step = jnp.stack([probe_sum.real / root, probe_sum.imag / root])
    return (specimen_grad, probe_step)
```

```python
import math

import jax
import jax.numpy as jnp
import numpy as np
from jax import lax
from jax.experimental import pallas as pl
from jax.experimental.pallas import tpu as pltpu
from jax.sharding import PartitionSpec as P

near_field = 0.25
LANES = 128
CHUNK = 32


def passed_along(value, axis, by):
    devices = lax.axis_size(axis)
    return lax.ppermute(value, axis, [(i, (i + by) % devices) for i in range(devices)])


def propagator_tables(width):
    index = np.arange(width)
    wave_number = np.where(index < width // 2, index, index - width)
    chirp = np.exp(-1j * math.pi * near_field * (wave_number**2 % (8 * width)) / width)
    kernel = np.fft.ifft(chirp)
    circulant = kernel[(index[:, None] - index[None, :]) % width]
    half = width // 2
    top, off = circulant[:half, :half], circulant[:half, half:]
    tables = []
    for part in ((top + off) / 2, (top - off) / 2):
        real, imag = part.real, part.imag
        forward = np.block([[real, imag], [-imag, real]]).astype(np.float32)
        for matrix in (forward, forward.T):
            high = matrix.astype(jnp.bfloat16)
            low = (matrix - high.astype(np.float32)).astype(jnp.bfloat16)
            tables.append((high, low))
    (sf, sb, df, db) = tables
    rights = np.stack([np.concatenate([h, h, l], axis=0) for h, l in (sf, df, sb, db)])
    lefts = np.stack([np.concatenate([h, h, l], axis=1) for h, l in (sb, db, sf, df)])
    return rights, lefts


def two_parts(value):
    high = value.astype(jnp.bfloat16)
    low = (value - high.astype(jnp.float32)).astype(jnp.bfloat16)
    return high, low


def window_kernel(
    width,
    offsets,
    live,
    specimen,
    low_a,
    low_b,
    side,
    corner,
    probe,
    measured,
    rights,
    lefts,
    own_out,
    right_out,
    low_a_out,
    low_b_out,
    corner_out,
    sums_out,
    ext,
    grad,
    obj,
    zs,
    zd,
    vs,
    vd,
    y_s,
    y_d,
    sem,
):
    tile = specimen.shape[1]
    half = width // 2
    blocks, wide = tile // LANES, width // LANES

    def pieces(buffer, own, a, b, right, diag, outward):
        copies = []
        for p in range(2):
            for j in range(blocks + wide):
                for rows, source in (
                    (pl.ds(0, tile), (own if j < blocks else right)),
                    (pl.ds(tile, width), ((a if j < wide else b) if j < blocks else diag)),
                ):
                    column = j if j < blocks else j - blocks
                    if source is b:
                        column = j - wide
                    far = source.at[p, :, pl.ds(column * LANES, LANES)]
                    near = buffer.at[p, j, rows, :]
                    copies.append(
                        pltpu.make_async_copy(near, far, sem)
                        if outward
                        else pltpu.make_async_copy(far, near, sem)
                    )
        return copies

    inward = pieces(ext, specimen, low_a, low_b, side, corner, False)
    for copy in inward:
        copy.start()

    @pl.loop(0, (tile + width) // CHUNK)
    def _(step):
        rows = pl.ds(pl.multiple_of(step * CHUNK, CHUNK), CHUNK)
        for p in range(2):
            for j in range(blocks + wide):
                grad[p, j, rows, :] = jnp.zeros((CHUNK, LANES), jnp.float32)

    sums_out[...] = jnp.zeros_like(sums_out)
    for copy in inward:
        copy.wait()
    lane = lax.broadcasted_iota(jnp.int32, (CHUNK, LANES), 1)

    def halves(array, *index):
        return array[(*index, pl.ds(0, LANES))], array[(*index, pl.ds(LANES, LANES))]

    def put_right(target, rows, first, second):
        for at, value in ((0, first), (LANES, second)):
            high, low = two_parts(value)
            target[rows, pl.ds(at, LANES)] = high
            target[rows, pl.ds(width + at, LANES)] = low
            target[rows, pl.ds(2 * width + at, LANES)] = high

    def put_left(target, row, count, at, value):
        high, low = two_parts(value)
        target[pl.ds(row, count), pl.ds(at, LANES)] = high
        target[pl.ds(width + row, count), pl.ds(at, LANES)] = low
        target[pl.ds(2 * width + row, count), pl.ds(at, LANES)] = high

    def product(left, right):
        return jnp.dot(left, right, preferred_element_type=jnp.float32)

    def slot(s, carry):
        row = offsets[2 * s]
        column = offsets[2 * s + 1]
        block = column // LANES
        shift = column - block * LANES
        back_shift = lax.rem(LANES - shift, LANES)
        keep = lane < LANES - shift
        placed = lane >= shift

        for k in range(0, width, CHUNK):
            rows = pl.ds(k, CHUNK)
            window = []
            for p in range(2):
                parts = [
                    pltpu.roll(ext[p, block + t, pl.ds(row + k, CHUNK), :], back_shift, 1)
                    for t in range(3)
                ]
                cut = (jnp.where(keep, parts[0], parts[1]), jnp.where(keep, parts[1], parts[2]))
                obj[p, rows, pl.ds(0, LANES)] = cut[0]
                obj[p, rows, pl.ds(LANES, LANES)] = cut[1]
                window.append(cut)
            psi_real, psi_imag = [], []
            for h in range(2):
                at = pl.ds(h * LANES, LANES)
                o_real, o_imag = window[0][h], window[1][h]
                p_real, p_imag = probe[0, rows, at], probe[1, rows, at]
                psi_real.append(p_real * o_real - p_imag * o_imag)
                psi_imag.append(p_real * o_imag + p_imag * o_real)
                sums_out[2, rows, at] += o_real * o_real + o_imag * o_imag
            put_right(zs, rows, psi_real[0] + psi_real[1], psi_imag[0] + psi_imag[1])
            put_right(zd, rows, psi_real[0] - psi_real[1], psi_imag[0] - psi_imag[1])

        y_s[...] = product(zs[...], rights[0])
        y_d[...] = product(zd[...], rights[1])
        for k in range(0, half, CHUNK):
            for at, y in ((0, y_s), (LANES, y_d)):
                for c in range(2):
                    top = y[pl.ds(k, CHUNK), pl.ds(c * LANES, LANES)]
                    bottom = y[pl.ds(half + k, CHUNK), pl.ds(c * LANES, LANES)]
                    put_left(vs, c * half + k, CHUNK, at, top + bottom)
                    put_left(vd, c * half + k, CHUNK, at, top - bottom)
        y_s[...] = product(lefts[0], vs[...])
        y_d[...] = product(lefts[1], vd[...])

        for k in range(0, half, CHUNK):
            wave = []
            for c in range(2):
                s_l, s_r = halves(y_s, pl.ds(c * half + k, CHUNK))
                d_l, d_r = halves(y_d, pl.ds(c * half + k, CHUNK))
                t_l, t_r, b_l, b_r = s_l + d_l, s_r + d_r, s_l - d_l, s_r - d_r
                wave.append(((t_l + t_r, t_l - t_r), (b_l + b_r, b_l - b_r)))
            for h in range(2):
                chi = []
                for v in range(2):
                    w_real, w_imag = wave[0][v][h], wave[1][v][h]
                    seen = measured[s, pl.ds(v * half + k, CHUNK), pl.ds(h * LANES, LANES)]
                    resid = w_real * w_real + w_imag * w_imag - seen
                    chi.append((resid * w_real, resid * w_imag))
                for c in range(2):
                    put_left(vs, c * half + k, CHUNK, h * LANES, chi[0][c] + chi[1][c])
                    put_left(vd, c * half + k, CHUNK, h * LANES, chi[0][c] - chi[1][c])
        y_s[...] = product(lefts[2], vs[...])
        y_d[...] = product(lefts[3], vd[...])
        for k in range(0, half, CHUNK):
            top, bottom = [], []
            for c in range(2):
                s_l, s_r = halves(y_s, pl.ds(c * half + k, CHUNK))
                d_l, d_r = halves(y_d, pl.ds(c * half + k, CHUNK))
                top.append((s_l + d_l, s_r + d_r))
                bottom.append((s_l - d_l, s_r - d_r))
            for start, part in ((k, top), (half + k, bottom)):
                rows = pl.ds(start, CHUNK)
                put_right(zs, rows, part[0][0] + part[0][1], part[1][0] + part[1][1])
                put_right(zd, rows, part[0][0] - part[0][1], part[1][0] - part[1][1])
        y_s[...] = product(zs[...], rights[2])
        y_d[...] = product(zd[...], rights[3])

        for k in range(0, width, CHUNK):
            rows = pl.ds(k, CHUNK)
            s_real, s_imag = halves(y_s, rows)
            d_real, d_imag = halves(y_d, rows)
            patch = ([], [])
            for h in range(2):
                at = pl.ds(h * LANES, LANES)
                b_real = s_real + d_real if h == 0 else s_real - d_real
                b_imag = s_imag + d_imag if h == 0 else s_imag - d_imag
                p_real, p_imag = probe[0, rows, at], probe[1, rows, at]
                o_real, o_imag = obj[0, rows, at], obj[1, rows, at]
                sums_out[0, rows, at] += o_real * b_real + o_imag * b_imag
                sums_out[1, rows, at] += o_real * b_imag - o_imag * b_real
                patch[0].append(pltpu.roll(p_real * b_real + p_imag * b_imag, shift, 1))
                patch[1].append(pltpu.roll(p_real * b_imag - p_imag * b_real, shift, 1))
            into = pl.ds(row + k, CHUNK)
            for p in range(2):
                left, right = patch[p]
                zero = jnp.zeros_like(left)
                grad[p, block, into, :] += jnp.where(placed, left, zero)
                grad[p, block + 1, into, :] += jnp.where(placed, right, left)
                grad[p, block + 2, into, :] += jnp.where(placed, zero, right)
        return carry

    lax.fori_loop(0, live[0], slot, 0)
    outward = pieces(grad, own_out, low_a_out, low_b_out, right_out, corner_out, True)
    for copy in outward:
        copy.start()
    for copy in outward:
        copy.wait()


def windows_gradient(specimen, low_a, low_b, side, corner, probe, measured, offsets, live):
    tile = specimen.shape[1]
    width = probe.shape[1]
    rights, lefts = propagator_tables(width)
    anywhere = pl.BlockSpec(memory_space=pl.ANY)
    vector = pl.BlockSpec(memory_space=pltpu.VMEM)
    scalar = pl.BlockSpec(memory_space=pltpu.SMEM)
    f32 = lambda *shape: jax.ShapeDtypeStruct(shape, jnp.float32)
    extended = (2, (tile + width) // LANES, tile + width, LANES)
    return pl.pallas_call(
        lambda *refs: window_kernel(width, *refs),
        out_shape=(
            f32(2, tile, tile),
            f32(2, tile, width),
            f32(2, width, width),
            f32(2, width, tile - width),
            f32(2, width, width),
            f32(3, width, width),
        ),
        in_specs=[scalar, scalar] + [anywhere] * 5 + [vector] * 4,
        out_specs=[anywhere] * 5 + [vector],
        scratch_shapes=[
            pltpu.VMEM(extended, jnp.float32),
            pltpu.VMEM(extended, jnp.float32),
            pltpu.VMEM((2, width, width), jnp.float32),
            pltpu.VMEM((width, 3 * width), jnp.bfloat16),
            pltpu.VMEM((width, 3 * width), jnp.bfloat16),
            pltpu.VMEM((3 * width, width), jnp.bfloat16),
            pltpu.VMEM((3 * width, width), jnp.bfloat16),
            pltpu.VMEM((width, width), jnp.float32),
            pltpu.VMEM((width, width), jnp.float32),
            pltpu.SemaphoreType.DMA,
        ],
        compiler_params=pltpu.CompilerParams(vmem_limit_bytes=48 * 2**20),
        name="windows",
    )(offsets, live, specimen, low_a, low_b, side, corner, probe, measured, jnp.asarray(rights), jnp.asarray(lefts))


def stages():
    columns = lax.axis_size("col")
    rows = lax.axis_size("row")
    found = [("col", 1, 2), ("row", 1, rows)]
    stride = 2
    while stride < columns:
        size = min(4, columns // stride)
        found.append(("col", stride, size))
        stride *= size
    return found


def swapped(value, axis, distance):
    devices = lax.axis_size(axis)
    return lax.ppermute(value, axis, [(i, i ^ distance) for i in range(devices)])


def total_rows(sums):
    for axis, stride, size in stages():
        count = sums.shape[1] // size
        place = lax.axis_index(axis) // stride % size
        piece = lambda m: lax.dynamic_slice_in_dim(sums, (place ^ m) * count, count, axis=1)
        received = [swapped(piece(m), axis, m * stride) for m in range(1, size)]
        total = piece(0)
        for value in received:
            total = total + value
        sums = total
    return sums


def all_rows(value):
    for axis, stride, size in reversed(stages()):
        count = value.shape[1]
        place = lax.axis_index(axis) // stride % size
        whole = jnp.zeros((value.shape[0], count * size, value.shape[2]), value.dtype)
        parts = [value] + [swapped(value, axis, m * stride) for m in range(1, size)]
        for m, part in enumerate(parts):
            whole = lax.dynamic_update_slice_in_dim(whole, part, (place ^ m) * count, axis=1)
        value = whole
    return value


def local(specimen, probe_field, measured, offsets, live_counts):
    width = probe_field.shape[1]
    low_a = passed_along(specimen[:, :width, :width], "row", -1)
    low_b = passed_along(specimen[:, :width, width:], "row", -1)
    side = passed_along(specimen[:, :, :width], "col", -1)
    corner = passed_along(low_a, "col", -1)
    own, right, back_a, back_b, diagonal, sums = windows_gradient(
        specimen,
        low_a,
        low_b,
        side,
        corner,
        probe_field,
        measured[0, 0],
        offsets.reshape(-1),
        live_counts.reshape(-1),
    )
    diagonal = passed_along(diagonal, "col", 1)
    back_b = passed_along(back_b, "row", 1)
    back_a = passed_along(back_a + diagonal, "row", 1)
    right = passed_along(right, "col", 1)
    sums = total_rows(sums)
    probe_step = all_rows(sums[:2] / jnp.sqrt(sums[2:]))
    top = jnp.concatenate([back_a + right[:, :width], back_b], axis=2)
    specimen_grad = own.at[:, :width, :].add(top).at[:, width:, :width].add(right[:, width:])
    return (specimen_grad, probe_step)


def solution(mesh):
    in_specs = (
        P(None, "row", "col"),
        P(),
        P("row", "col", None, None, None),
        P("row", "col", None, None),
        P("row", "col"),
    )
    out_specs = (P(None, "row", "col"), P())
    return jax.shard_map(local, mesh=mesh, in_specs=in_specs, out_specs=out_specs, check_vma=False)
```
